32 devices in a mesh: groups: 2 (over x), frame: 8 (over z, y), tok: 2 (over core).
Axes of the slice: x: 2, y: 2, z: 4, core: 2. Of those that a mesh axis runs over, the one named last changes fastest.
Arguments:
- video: bfloat16 [32, 512, 1152], P(('groups', 'frame'), 'tok'), parts along dimension 0, may hold values from -6 to 6
- regions: int32 [32, 512], P(('groups', 'frame'), 'tok'), parts along dimension 0, may hold values from 0 to 2
- prev_frame: int32 [32], P('groups'), parts along dimension 0, may hold values from 0 to 14, as said below
- gain_spatial: float32 [1152], replicated, may hold values from 0.7 to 4
- qkv_spatial: bfloat16 [1152, 3456], replicated, may hold values from -0.35355339 to 0.35355339
- out_spatial: bfloat16 [1152, 1152], replicated, may hold values from -1.5 to 1.5
- gain_temporal: float32 [1152], replicated, may hold values from 0.7 to 4
- qkv_temporal: bfloat16 [1152, 3456], replicated, may hold values from -0.35355339 to 0.35355339
- out_temporal: bfloat16 [1152, 1152], replicated, may hold values from -0.75 to 0.75
Outputs:
- result: bfloat16 [32, 512, 1152], P(('groups', 'frame'), 'tok'), parts along dimension 0
The draws below stay inside these ranges and needn't reach their ends.
There are 2 independent parts, one for each index of `groups`. The reference program is written for one: setup_inputs(seed, part) draws one part's arguments, and reference() takes and returns one part's arrays. A program takes and returns all parts, laid end to end along the dimension named above; an argument that names none is the same for every part. Nothing has to cross between parts.
Inputs may be any that keep to these rules, and one draw needn't show every extreme that they name: prev_frame[f] is f - 1 or f - 2 for 2 <= f < 15, f - 1 for f = 15, and 0 for f < 2.
All inputs are finite; a program needn't handle non-finite values.
Results may differ from the reference program's by a relative error of at most 0.014.
The reference program's roundings to bfloat16 on the way count: a program that leaves them out, or rounds other values in their place, can miss the bound.
Values may be sent and summed in bfloat16 or wider, within the bound.
No kernel may reach another device: no remote copies, remote signals or barrier semaphores. Data moves between devices by JAX's collectives and lax.ppermute only.
A program may use at most 192 MiB of HBM per device.

```python
import jax
import jax.numpy as jnp
from jax import lax

HEADS = 16
HEAD_DIM = 72
D = 1152
FRAMES = 16
PLACES = 512


def draw_prev_frame(key, part):
    frame_number = jnp.arange(FRAMES, dtype=jnp.int32)
    skipped = jax.random.randint(jax.random.fold_in(key, 7), (FRAMES,), 0, 2, dtype=jnp.int32)
    skipped = jnp.where(frame_number == FRAMES - 1, 0, skipped)
    return jnp.maximum(frame_number - 1 - skipped, 0).astype(jnp.int32)


def gain_draw(key, salt):
    return jax.random.uniform(jax.random.fold_in(key, salt + 4), (D,), jnp.float32, 0.7, 1.3)


def projection_draw(key, salt):
    base = jax.random.truncated_normal(jax.random.fold_in(key, salt + 2), -6.0, 6.0, (D, 3 * D), jnp.float32)
    base = base * D ** (-0.5)
    return base.astype(jnp.bfloat16)


def draw_gain_spatial(key, part):
    return gain_draw(key, 11)


def draw_qkv_spatial(key, part):
    return projection_draw(key, 11)


def draw_gain_temporal(key, part):
    return gain_draw(key, 31)


def draw_qkv_temporal(key, part):
    return projection_draw(key, 31)


def with_ends(values, stream_key, smallest, high):
    longest = values.shape.index(max(values.shape))
    spots = []
    for shift in (0, 1):
        where = [jax.random.randint(jax.random.fold_in(stream_key, axis), (), 0, length) for axis, length in enumerate(values.shape)]
        where[longest] = (where[longest] + shift) % values.shape[longest]
        spots.append(tuple(where))
    return values.at[spots[0]].set(smallest).at[spots[1]].set(high)


def block_levels(key, dims, split, smallest, high):
    def one(dim, blocks):
        heights = jax.random.uniform(jax.random.fold_in(jax.random.fold_in(key, 6), dim), (blocks,), jnp.float32, smallest / len(split), high / len(split))
        return jnp.repeat(jnp.exp(heights), dims[dim] // blocks).reshape((-1,) + (1,) * (len(dims) - dim - 1))

    factor_of = one(*split[0])
    for cut in split[1:]:
        factor_of = factor_of * one(*cut)
    return factor_of


def gaussian(key, extent, deviation, bound, pieces=(), kind=jnp.bfloat16):
    drawn = jax.random.normal(key, extent, jnp.float32) * deviation
    if len(pieces) > 0:
        drawn = block_levels(key, extent, pieces, -0.22, 0.18) * drawn
    return jnp.clip(drawn, min=-bound, max=bound).astype(kind)


def setup_inputs(seed: int = 0, part: int = 0) -> dict:
    arg_keys = jax.random.split(jax.random.key(seed), 10)
    own_keys = jax.random.split(jax.random.fold_in(arg_keys[9], part), 10)
    return {
        "video": gaussian(own_keys[0], (FRAMES, PLACES, D), 1.0, 6.0, ((0, 8), (1, 2))),
        "regions": with_ends(jax.random.randint(own_keys[1], (FRAMES, PLACES), 0, 3), jax.random.fold_in(own_keys[1], 1), 0, 2).astype(jnp.int32),
        "prev_frame": draw_prev_frame(jax.random.fold_in(jax.random.fold_in(arg_keys[9], part), 71), part),
        "gain_spatial": draw_gain_spatial(jax.random.fold_in(arg_keys[9], 71), part),
        "qkv_spatial": draw_qkv_spatial(jax.random.fold_in(arg_keys[9], 71), part),
        "out_spatial": gaussian(arg_keys[5], (D, D), (max(D // 64, 1)) ** -0.5, 1.5),
        "gain_temporal": draw_gain_temporal(jax.random.fold_in(arg_keys[9], 71), part),
        "qkv_temporal": draw_qkv_temporal(jax.random.fold_in(arg_keys[9], 71), part),
        "out_temporal": gaussian(arg_keys[8], (D, D), (max(D // 16, 1)) ** -0.5, 0.75),
    }


def layer_norm(row_data, gain_vector):
    values = row_data.astype(jnp.float32)
    center = values - lax.optimization_barrier(jnp.mean(values, axis=-1, keepdims=True))
    spread = lax.optimization_barrier(jnp.mean(center * center, axis=-1, keepdims=True))
    return (center * lax.rsqrt(spread + 1e-06) * gain_vector).astype(jnp.bfloat16)

def softmax_rows(scores, visible):
    masked = jnp.where(visible, scores, -jnp.inf)
    largest = lax.optimization_barrier(jnp.max(masked, axis=-1, keepdims=True))
    exponent = jnp.exp(masked - largest)
    return (exponent / lax.optimization_barrier(jnp.sum(exponent, axis=-1, keepdims=True))).astype(jnp.bfloat16)

def reference(video, regions, prev_frame, gain_spatial, qkv_spatial, out_spatial, gain_temporal, qkv_temporal, out_temporal):
    frame_total, places, feature = video.shape
    score_scale = HEAD_DIM ** (-0.5)
    row_count = frame_total * places
    normed = layer_norm(video.reshape(row_count, feature), gain_spatial)
    packed = jnp.dot(normed, qkv_spatial, preferred_element_type=jnp.float32).astype(jnp.bfloat16)
    packed = packed.reshape(frame_total, places, 3, HEADS, HEAD_DIM)
    queries = packed[:, :, 0].astype(jnp.float32)
    keys_all = packed[:, :, 1].astype(jnp.float32)
    values_all = packed[:, :, 2].astype(jnp.float32)
    keep_flag = regions == 0

    def attend_frame(frame_number):
        back_frame = prev_frame[frame_number]
        key_rows = jnp.concatenate([keys_all[frame_number], keys_all[0], keys_all[back_frame]], axis=0)
        value_rows = jnp.concatenate([values_all[frame_number], values_all[0], values_all[back_frame]], axis=0)
        visible = jnp.concatenate([jnp.ones((places,), jnp.bool_), keep_flag[0], keep_flag[back_frame]])
        scores = jnp.einsum('qhd,khd->hqk', queries[frame_number], key_rows) * score_scale
        weights = softmax_rows(scores, visible[None, None, :]).astype(jnp.float32)
        return jnp.einsum('hqk,khd->qhd', weights, value_rows).astype(jnp.bfloat16)
    attended = lax.map(attend_frame, jnp.arange(frame_total, dtype=jnp.int32)).reshape(row_count, feature)
    mixed_rows = (video.reshape(row_count, feature).astype(jnp.float32) + jnp.dot(attended, out_spatial, preferred_element_type=jnp.float32)).astype(jnp.bfloat16)
    normed_t = layer_norm(mixed_rows, gain_temporal)
    packed_t = jnp.dot(normed_t, qkv_temporal, preferred_element_type=jnp.float32).astype(jnp.bfloat16)
    packed_t = packed_t.reshape(frame_total, places, 3, HEADS, HEAD_DIM)
    query_t = packed_t[:, :, 0].astype(jnp.float32)
    key_t = packed_t[:, :, 1].astype(jnp.float32)
    value_t = packed_t[:, :, 2].astype(jnp.float32)
    scores_t = jnp.einsum('fphd,gphd->phfg', query_t, key_t) * score_scale
    open_flag = (regions != 2).T
    visible_t = open_flag[:, None, None, :] | jnp.eye(frame_total, dtype=jnp.bool_)[None, None]
    weights_t = softmax_rows(scores_t, visible_t).astype(jnp.float32)
    temporal_out = jnp.einsum('phfg,gphd->fphd', weights_t, value_t).astype(jnp.bfloat16).reshape(row_count, feature)
    result = (mixed_rows.astype(jnp.float32) + jnp.dot(temporal_out, out_temporal, preferred_element_type=jnp.float32)).astype(jnp.bfloat16)
    return result.reshape(frame_total, places, feature)
```

```python
import functools

import jax
import jax.numpy as jnp
from jax import lax
from jax.experimental import pallas as pl
from jax.experimental.pallas import tpu as pltpu
from jax.sharding import PartitionSpec as P

HEADS = 16
WINDOW = 256
LANES = 128
PIECE_ROWS = 16
LOG2E = 1.4426950408889634


def vmem():
    return pl.BlockSpec(memory_space=pltpu.VMEM)


def params(*semantics):
    return pltpu.CompilerParams(
        dimension_semantics=semantics or None, vmem_limit_bytes=56 << 20
    )


def norm_rows(src_ref, gain_ref, dst_ref, block=32):
    rows, feature = src_ref.shape
    gain = gain_ref[...]

    def step(r, carry):
        at = pl.ds(pl.multiple_of(r * block, block), block)
        values = src_ref[at, :].astype(jnp.float32)
        center = values - jnp.mean(values, axis=-1, keepdims=True)
        spread = jnp.mean(center * center, axis=-1, keepdims=True)
        dst_ref[at, :] = (center * lax.rsqrt(spread + 1e-06) * gain).astype(jnp.bfloat16)
        return carry

    lax.fori_loop(0, rows // block, step, 0)


def project(src_ref, weight_ref, w_off, dst_ref, width):
    full = width // WINDOW

    def step(j, carry):
        at = pl.multiple_of(j * WINDOW, WINDOW)
        dst_ref[:, pl.ds(at, WINDOW)] = jnp.dot(
            src_ref[...],
            weight_ref[:, pl.ds(pl.multiple_of(w_off + at, LANES), WINDOW)],
            preferred_element_type=jnp.float32,
        ).astype(jnp.bfloat16)
        return carry

    lax.fori_loop(0, full, step, 0)
    rest = width - full * WINDOW
    if rest:
        dst_ref[:, full * WINDOW : width] = jnp.dot(
            src_ref[...],
            weight_ref[:, w_off + full * WINDOW : w_off + width],
            preferred_element_type=jnp.float32,
        ).astype(jnp.bfloat16)


def head_window(h, head_size, feature):
    start = jnp.minimum((h * head_size) // LANES * LANES, feature - WINDOW)
    start = pl.multiple_of(start, LANES)
    lane = start + lax.broadcasted_iota(jnp.int32, (1, WINDOW), 1)
    inside = (lane >= h * head_size) & (lane < (h + 1) * head_size)
    return start, inside


def heads_loop(body, unroll=2):
    def step(g, carry):
        for u in range(unroll):
            body(g * unroll + u)
        return carry

    lax.fori_loop(0, HEADS // unroll, step, 0)


def pick(column_ref, h):
    lane = lax.broadcasted_iota(jnp.int32, (1, LANES), 1)
    return jnp.sum(jnp.where(lane == h, column_ref[...], 0.0), axis=-1, keepdims=True)


def put(column_ref, h, value):
    lane = lax.broadcasted_iota(jnp.int32, (1, LANES), 1)
    column_ref[...] = jnp.where(lane == h, value, column_ref[...])


def scores_of(query, key):
    return lax.dot_general(
        query, key, (((1,), (1,)), ((), ())), preferred_element_type=jnp.float32
    )


def attend(q_ref, k_ref, v_ref, bias, state, out, feature):
    head_size = feature // HEADS
    rate = head_size ** (-0.5) * LOG2E
    (m_in, m_out), (l_in, l_out), (acc_in, acc_out) = state

    def body(h):
        start, inside = head_window(h, head_size, feature)
        at = pl.ds(start, WINDOW)
        query = jnp.where(inside, q_ref[:, at], 0).astype(jnp.bfloat16)
        scores = scores_of(query, k_ref[:, at])
        if bias is not None:
            scores = scores + bias
        top = jnp.max(scores, axis=-1, keepdims=True)
        if m_in is not None:
            before = pick(m_in, h)
            top = jnp.maximum(top, before)
            fade = jnp.exp2((before - top) * rate)
        weight = jnp.exp2((scores - top) * rate)
        total = jnp.sum(weight, axis=-1, keepdims=True)
        mixed = jnp.dot(
            weight.astype(jnp.bfloat16), v_ref[:, at], preferred_element_type=jnp.float32
        )
        if m_in is not None:
            total = total + pick(l_in, h) * fade
            mixed = mixed + acc_in[:, at] * fade
        if out is not None:
            done = (mixed * (1.0 / total)).astype(jnp.bfloat16)
            out[:, at] = jnp.where(inside, done, out[:, at])
        else:
            put(m_out, h, top)
            put(l_out, h, total)
            acc_out[:, at] = jnp.where(inside, mixed, acc_out[:, at])

    heads_loop(body)


def own_kernel(xa_ref, xb_ref, gain_ref, w_ref, q_ref, m_ref, l_ref, acc_ref, normed, kv):
    half, feature = xa_ref.shape
    norm_rows(xa_ref, gain_ref, normed.at[:half])
    norm_rows(xb_ref, gain_ref, normed.at[half:])
    project(normed.at[:half], w_ref, 0, q_ref, feature)
    project(normed, w_ref, feature, kv, 2 * feature)
    attend(
        q_ref,
        kv.at[:, :feature],
        kv.at[:, feature:],
        None,
        ((None, m_ref), (None, l_ref), (None, acc_ref)),
        None,
        feature,
    )


def own_segment(x_own, x_par, gain, weight):
    frames, half, feature = x_own.shape
    per_frame = pl.BlockSpec((None, half, feature), lambda f: (f, 0, 0))
    column = pl.BlockSpec((None, half, LANES), lambda f: (f, 0, 0))
    return pl.pallas_call(
        own_kernel,
        name="own_segment",
        grid=(frames,),
        in_specs=[per_frame, per_frame, vmem(), vmem()],
        out_specs=[per_frame, column, column, per_frame],
        out_shape=[
            jax.ShapeDtypeStruct((frames, half, feature), jnp.bfloat16),
            jax.ShapeDtypeStruct((frames, half, LANES), jnp.float32),
            jax.ShapeDtypeStruct((frames, half, LANES), jnp.float32),
            jax.ShapeDtypeStruct((frames, half, feature), jnp.float32),
        ],
        scratch_shapes=[
            pltpu.VMEM((2 * half, feature), jnp.bfloat16),
            pltpu.VMEM((2 * half, 2 * feature), jnp.bfloat16),
        ],
        compiler_params=params("arbitrary"),
    )(x_own, x_par, gain, weight)


def prev_kernel(
    count,
    slot_ref,
    *refs,
):
    sources = refs[: 2 * count]
    (gain_ref, w_ref, bias_ref, q_ref, m_in, l_in, acc_in) = refs[2 * count : 2 * count + 7]
    (m_ref, l_ref, acc_ref, rows, normed, kv, sem) = refs[2 * count + 7 :]
    half, feature = q_ref.shape
    slot = slot_ref[pl.program_id(0)]
    for s in range(count):

        @pl.when(slot == s)
        def _(s=s):
            copies = [
                pltpu.make_async_copy(sources[2 * s + t], rows.at[t * half : (t + 1) * half], sem.at[t])
                for t in range(2)
            ]
            for copy in copies:
                copy.start()
            for copy in copies:
                copy.wait()

    norm_rows(rows, gain_ref, normed)
    project(normed, w_ref, feature, kv, 2 * feature)
    attend(
        q_ref,
        kv.at[:, :feature],
        kv.at[:, feature:],
        bias_ref[...],
        ((m_in, m_ref), (l_in, l_ref), (acc_in, acc_ref)),
        None,
        feature,
    )


def prev_segment(slot, sources, gain, weight, bias, q, m, l, acc):
    frames, half, feature = q.shape
    keys = bias.shape[-1]
    per_frame = pl.BlockSpec((None, half, feature), lambda f, s: (f, 0, 0))
    column = pl.BlockSpec((None, half, LANES), lambda f, s: (f, 0, 0))
    return pl.pallas_call(
        functools.partial(prev_kernel, len(sources) // 2),
        name="prev_segment",
        grid_spec=pltpu.PrefetchScalarGridSpec(
            num_scalar_prefetch=1,
            grid=(frames,),
            in_specs=[pl.BlockSpec(memory_space=pl.ANY)] * len(sources)
            + [
                vmem(),
                vmem(),
                pl.BlockSpec((None, 1, keys), lambda f, s: (f, 0, 0)),
                per_frame,
                column,
                column,
                per_frame,
            ],
            out_specs=[column, column, per_frame],
            scratch_shapes=[
                pltpu.VMEM((keys, feature), jnp.bfloat16),
                pltpu.VMEM((keys, feature), jnp.bfloat16),
                pltpu.VMEM((keys, 2 * feature), jnp.bfloat16),
                pltpu.SemaphoreType.DMA((2,)),
            ],
        ),
        out_shape=[
            jax.ShapeDtypeStruct(m.shape, jnp.float32),
            jax.ShapeDtypeStruct(l.shape, jnp.float32),
            jax.ShapeDtypeStruct(acc.shape, jnp.float32),
        ],
        compiler_params=params("arbitrary"),
    )(slot, *sources, gain, weight, bias, q, m, l, acc)


def first_kv_kernel(xa_ref, xb_ref, gain_ref, w_ref, kv_ref, normed):
    half = xa_ref.shape[0]

    @pl.when(pl.program_id(0) == 0)
    def _():
        norm_rows(xa_ref, gain_ref, normed.at[:half])
        norm_rows(xb_ref, gain_ref, normed.at[half:])

    kv_ref[...] = jnp.dot(
        normed[...], w_ref[...], preferred_element_type=jnp.float32
    ).astype(jnp.bfloat16)


def first_kv(xa, xb, gain, weight):
    half, feature = xa.shape
    block = 3 * LANES
    lead = feature // block
    return pl.pallas_call(
        first_kv_kernel,
        name="first_kv",
        grid=(2 * feature // block,),
        in_specs=[
            vmem(),
            vmem(),
            vmem(),
            pl.BlockSpec((feature, block), lambda j: (0, lead + j)),
        ],
        out_specs=pl.BlockSpec((2 * half, block), lambda j: (0, j)),
        out_shape=jax.ShapeDtypeStruct((2 * half, 2 * feature), jnp.bfloat16),
        scratch_shapes=[pltpu.VMEM((2 * half, feature), jnp.bfloat16)],
        compiler_params=params("arbitrary"),
    )(xa, xb, gain, weight)


def last_kernel(
    me_ref, kv_ref, bias_ref, q_ref, m_ref, l_ref, acc_ref, x_ref, w_ref, *refs
):
    parties = x_ref.shape[1]
    frames, _, piece, feature = x_ref.shape
    outs = refs[:parties]
    q_rows, m_rows, l_rows, acc_rows, att, mixed = refs[parties:]
    rows = frames * parties * piece
    q_rows[...] = q_ref[...].reshape(rows, feature)
    m_rows[...] = m_ref[...].reshape(rows, LANES)
    l_rows[...] = l_ref[...].reshape(rows, LANES)
    acc_rows[...] = acc_ref[...].reshape(rows, feature)
    attend(
        q_rows,
        kv_ref.at[:, :feature],
        kv_ref.at[:, feature:],
        bias_ref[...],
        ((m_rows, None), (l_rows, None), (acc_rows, None)),
        att,
        feature,
    )
    total = x_ref[...].reshape(rows, feature).astype(jnp.float32) + jnp.dot(
        att[...], w_ref[...], preferred_element_type=jnp.float32
    )
    mixed[...] = total.astype(jnp.bfloat16).reshape(frames, parties, piece, feature)
    me = me_ref[0]
    for k in range(parties):
        outs[k][...] = mixed[:, lax.rem(me + k, parties)]


def last_segment(me, kv, bias, q, m, l, acc, x, weight, parties, piece, chunk):
    frames, half, feature = q.shape
    chunks = half // (parties * piece)
    rows = frames * parties * piece

    def split(array):
        return array.reshape(frames, parties, chunks, piece, array.shape[-1])

    def spec(width):
        return pl.BlockSpec(
            (frames, parties, None, piece, width), lambda g, me: (0, 0, chunk, 0, 0)
        )

    return pl.pallas_call(
        last_kernel,
        name="last_segment",
        grid_spec=pltpu.PrefetchScalarGridSpec(
            num_scalar_prefetch=1,
            grid=(1,),
            in_specs=[vmem(), vmem(), spec(feature), spec(LANES), spec(LANES), spec(feature)]
            + [spec(feature), vmem()],
            out_specs=[vmem()] * parties,
            scratch_shapes=[
                pltpu.VMEM((rows, feature), jnp.bfloat16),
                pltpu.VMEM((rows, LANES), jnp.float32),
                pltpu.VMEM((rows, LANES), jnp.float32),
                pltpu.VMEM((rows, feature), jnp.float32),
                pltpu.VMEM((rows, feature), jnp.bfloat16),
                pltpu.VMEM((frames, parties, piece, feature), jnp.bfloat16),
            ],
        ),
        out_shape=[jax.ShapeDtypeStruct((frames, piece, feature), jnp.bfloat16)] * parties,
        compiler_params=params("arbitrary"),
    )(me, kv, bias, split(q), split(m), split(l), split(acc), split(x), weight)


def temporal_kernel(parties, *refs):
    pieces = refs[:parties]
    open_ref, gain_ref, w_ref, out_w_ref = refs[parties : parties + 4]
    outs = refs[parties + 4 : 2 * parties + 4]
    rows_ref, normed, packed, bias, mix, w_buf, o_buf, sem = refs[2 * parties + 4 :]
    frames, piece, feature = pieces[0].shape
    head_size = feature // HEADS
    rate = head_size ** (-0.5) * LOG2E
    rows = parties * frames * piece
    copies = [
        pltpu.make_async_copy(
            w_ref.at[:, s * feature : (s + 1) * feature], w_buf.at[s], sem.at[s]
        )
        for s in range(3)
    ] + [pltpu.make_async_copy(out_w_ref, o_buf, sem.at[3])]
    for copy in copies:
        copy.start()
    step = frames * piece
    for k in range(parties):
        rows_ref[k * step : (k + 1) * step, :] = pieces[k][...].reshape(step, feature)
    norm_rows(rows_ref, gain_ref, normed)
    row = lax.broadcasted_iota(jnp.int32, (rows, rows), 0)
    column = lax.broadcasted_iota(jnp.int32, (rows, rows), 1)
    same_place = (row & (piece - 1)) == (column & (piece - 1))
    seen = same_place & ((row == column) | (open_ref[...] > 0))
    bias[...] = jnp.where(seen, 0.0, -jnp.inf)
    for s in range(3):
        copies[s].wait()
        project(normed, w_buf.at[s], 0, packed.at[s], feature)

    def body(h):
        start, inside = head_window(h, head_size, feature)
        at = pl.ds(start, WINDOW)
        query = jnp.where(inside, packed[0, :, at], 0).astype(jnp.bfloat16)
        scores = scores_of(query, packed[1, :, at]) + bias[...]
        top = jnp.max(scores, axis=-1, keepdims=True)
        weight = jnp.exp2((scores - top) * rate)
        total = jnp.sum(weight, axis=-1, keepdims=True)
        got = jnp.dot(
            weight.astype(jnp.bfloat16), packed[2, :, at], preferred_element_type=jnp.float32
        )
        done = (got * (1.0 / total)).astype(jnp.bfloat16)
        mix[:, at] = jnp.where(inside, done, mix[:, at])

    heads_loop(body)
    copies[3].wait()
    result = rows_ref[...].astype(jnp.float32) + jnp.dot(
        mix[...], o_buf[...], preferred_element_type=jnp.float32
    )
    result = result.astype(jnp.bfloat16)
    for k in range(parties):
        outs[k][...] = result[k * step : (k + 1) * step, :].reshape(frames, piece, feature)


def temporal_block(pieces, open_row, gain, weight, out_weight):
    parties = len(pieces)
    frames, piece, feature = pieces[0].shape
    rows = parties * frames * piece
    return pl.pallas_call(
        functools.partial(temporal_kernel, parties),
        name="temporal_block",
        in_specs=[vmem()] * (parties + 2) + [pl.BlockSpec(memory_space=pl.ANY)] * 2,
        out_specs=[vmem()] * parties,
        out_shape=[jax.ShapeDtypeStruct((frames, piece, feature), jnp.bfloat16)] * parties,
        scratch_shapes=[
            pltpu.VMEM((rows, feature), jnp.bfloat16),
            pltpu.VMEM((rows, feature), jnp.bfloat16),
            pltpu.VMEM((3, rows, feature), jnp.bfloat16),
            pltpu.VMEM((rows, rows), jnp.float32),
            pltpu.VMEM((rows, feature), jnp.bfloat16),
            pltpu.VMEM((3, feature, feature), jnp.bfloat16),
            pltpu.VMEM((feature, feature), jnp.bfloat16),
            pltpu.SemaphoreType.DMA((4,)),
        ],
        compiler_params=params(),
    )(*pieces, open_row, gain, weight, out_weight)


def gather_kernel(chunks, parties, me_ref, *refs):
    out_ref = refs[-1]
    me = me_ref[0]
    for c in range(chunks):
        for k in range(parties):
            out_ref[:, lax.rem(me + k, parties), c] = refs[c * parties + k][...]


def gather_pieces(me, pieces, chunks, parties):
    frames, piece, feature = pieces[0].shape
    shape = (frames, parties, chunks, piece, feature)
    out = pl.pallas_call(
        functools.partial(gather_kernel, chunks, parties),
        name="gather_pieces",
        in_specs=[pl.BlockSpec(memory_space=pltpu.SMEM)] + [vmem()] * len(pieces),
        out_specs=vmem(),
        out_shape=jax.ShapeDtypeStruct(shape, jnp.bfloat16),
        compiler_params=params(),
    )(me, *pieces)
    return out.reshape(frames, parties * chunks * piece, feature)


def swap(array, axis):
    count = lax.axis_size(axis)
    return lax.ppermute(array, axis, [(i, count - 1 - i) for i in range(count)])


def shards(
    video,
    regions,
    prev_frame,
    gain_spatial,
    qkv_spatial,
    out_spatial,
    gain_temporal,
    qkv_temporal,
    out_temporal,
):
    frames, half, feature = video.shape
    parties = lax.axis_size("frame")
    toks = lax.axis_size("tok")
    me = lax.axis_index("frame")
    tok = lax.axis_index("tok")
    gain_s = gain_spatial.reshape(1, feature)
    gain_t = gain_temporal.reshape(1, feature)
    me_arr = me.reshape(1).astype(jnp.int32)

    x_par = swap(video, "tok")
    forward = [(i, i + 1) for i in range(parties - 1)]
    tail = [lax.ppermute(video[f], "frame", forward) for f in range(frames)]

    def spread_from(value, offset):
        stride = parties // 2
        while stride >= 2:
            pairs = [
                (j + offset, j + offset + stride) for j in range(0, parties, 2 * stride)
            ]
            got = lax.ppermute(value, "frame", pairs)
            takes = functools.reduce(jnp.logical_or, [me == d for _, d in pairs])
            value = jnp.where(takes, got, value)
            stride //= 2
        return value

    even = spread_from(video[0], 0)
    odd = spread_from(tail[0], 1) if parties > 1 else even
    x_first = jnp.where(me % 2 == 0, even, odd)
    tail_par = [swap(t, "tok") for t in tail]
    first_par = swap(x_first, "tok")

    region_bits = regions.astype(jnp.float32)
    copies = jnp.broadcast_to(region_bits[None], (parties * toks, frames, half))
    every = lax.all_to_all(copies, ("frame", "tok"), split_axis=0, concat_axis=0, tiled=True)
    every = every.reshape(parties, toks, frames, half).transpose(0, 2, 1, 3)
    every = every.reshape(parties * frames, toks, half)
    mine_first = jnp.where(tok == 0, every, every[:, ::-1])
    keep_bias = jnp.where(mine_first == 0, 0.0, -jnp.inf).astype(jnp.float32)
    keep_bias = keep_bias.reshape(parties * frames, 1, toks * half)

    first_index = me * frames
    table_index = jnp.arange(prev_frame.shape[0], dtype=jnp.int32)
    own_frames = first_index + jnp.arange(frames, dtype=jnp.int32)
    picked = jnp.sum(
        jnp.where(table_index[None, :] == own_frames[:, None], prev_frame[None, :], 0), axis=1
    )
    slot = (picked - first_index + frames).astype(jnp.int32)
    prev_bias = jnp.take(keep_bias, picked, axis=0)

    q, m, l, acc = own_segment(video, x_par, gain_s, qkv_spatial)
    sources = []
    for s in range(frames):
        sources += [tail[s], tail_par[s]]
    sources += [video[0], x_par[0]]
    m, l, acc = prev_segment(slot, sources, gain_s, qkv_spatial, prev_bias, q, m, l, acc)
    kv = first_kv(x_first, first_par, gain_s, qkv_spatial)

    chunks = half // (parties * PIECE_ROWS)
    my_places = lax.dynamic_slice_in_dim(mine_first[:, 0], me * (half // parties), half // parties, 1)
    my_open = (my_places != 2).astype(jnp.float32).reshape(parties, frames, chunks, PIECE_ROWS)
    order = (me - jnp.arange(parties, dtype=jnp.int32)) % parties
    my_open = jnp.take(my_open, order, axis=0)

    shift = lambda a, k: lax.ppermute(
        a, "frame", [(j, (j + k) % parties) for j in range(parties)]
    )
    returned = []
    for c in range(chunks):
        sent = last_segment(
            me_arr, kv, keep_bias[0], q, m, l, acc, video, out_spatial, parties, PIECE_ROWS, c
        )
        got = [sent[0]] + [shift(sent[k], k) for k in range(1, parties)]
        open_row = my_open[:, :, c].reshape(1, -1)
        back = temporal_block(got, open_row, gain_t, qkv_temporal, out_temporal)
        returned += [back[0]] + [shift(back[k], -k) for k in range(1, parties)]
    return gather_pieces(me_arr, returned, chunks, parties)


def solution(mesh):
    placed = (
        P(("groups", "frame"), "tok", None),
        P(("groups", "frame"), "tok"),
        P("groups"),
        P(),
        P(),
        P(),
        P(),
        P(),
        P(),
    )
    return jax.shard_map(
        shards,
        mesh=mesh,
        in_specs=placed,
        out_specs=P(("groups", "frame"), "tok", None),
        check_vma=False,
    )
```

```python
import functools

import jax
import jax.numpy as jnp
from jax import lax
from jax.experimental import pallas as pl
from jax.experimental.pallas import tpu as pltpu
from jax.sharding import PartitionSpec as P


HEADS = 16
BLOCK = 256
GROUP = 4
COLUMNS = 768
LANES = 128
PIECE_ROWS = 16
STAMP = 16
LOG2E = 1.4426950408889634


def vmem():
    return pl.BlockSpec(memory_space=pltpu.VMEM)


def whole():
    return pl.BlockSpec(memory_space=pl.ANY)


def params(*semantics):
    return pltpu.CompilerParams(
        dimension_semantics=semantics or None, vmem_limit_bytes=56 << 20
    )


def cost(flops, moved):
    return pl.CostEstimate(flops=flops, transcendentals=0, bytes_accessed=moved)


def norm_rows(src_ref, gain_ref, dst_ref, block=32):
    rows, _ = src_ref.shape
    gain = gain_ref[...]

    def step(r, carry):
        at = pl.ds(pl.multiple_of(r * block, block), block)
        values = src_ref[at, :].astype(jnp.float32)
        center = values - jnp.mean(values, axis=-1, keepdims=True)
        spread = jnp.mean(center * center, axis=-1, keepdims=True)
        dst_ref[at, :] = (center * lax.rsqrt(spread + 1e-06) * gain).astype(jnp.bfloat16)
        return carry

    lax.fori_loop(0, rows // block, step, 0, unroll=4)


def project(src_ref, weight_ref, dst_ref):
    width = dst_ref.shape[1]
    for at in range(0, width, COLUMNS):
        stop = min(at + COLUMNS, width)
        dst_ref[:, at:stop] = jnp.dot(
            src_ref[...], weight_ref[:, at:stop], preferred_element_type=jnp.float32
        ).astype(jnp.bfloat16)


def window(h, head_size):
    low, high = h * head_size, (h + 1) * head_size
    start = low // LANES * LANES
    stop = pl.cdiv(high, LANES) * LANES
    lane = start + lax.broadcasted_iota(jnp.int32, (1, stop - start), 1)
    return slice(start, stop), (lane >= low) & (lane < high)


def scores_of(query, key):
    return lax.dot_general(
        query, key, (((1,), (1,)), ((), ())), preferred_element_type=jnp.float32
    )


def head_groups(body):
    for first in range(0, HEADS, GROUP):
        body(range(first, first + GROUP))


def attend(q_ref, k_ref, v_ref, bias, m_ref, l_ref, acc_ref):
    head_size = q_ref.shape[1] // HEADS
    rate = head_size ** (-0.5) * LOG2E
    lane = lax.broadcasted_iota(jnp.int32, (1, LANES), 1)

    def body(heads):
        views = [window(h, head_size) for h in heads]
        scores = [
            scores_of(jnp.where(own, q_ref[:, at], 0).astype(jnp.bfloat16), k_ref[:, at])
            for at, own in views
        ]
        if bias is not None:
            scores = [s + bias for s in scores]
        tops = [jnp.max(s, axis=-1, keepdims=True) for s in scores]
        weights = [jnp.exp2((s - t) * rate) for s, t in zip(scores, tops)]
        totals = [jnp.sum(w, axis=-1, keepdims=True) for w in weights]
        mixes = [
            jnp.dot(w.astype(jnp.bfloat16), v_ref[:, at], preferred_element_type=jnp.float32)
            for w, (at, _) in zip(weights, views)
        ]
        for i, h in enumerate(heads):
            at, own = views[i]
            m_ref[...] = jnp.where(lane == h, tops[i], m_ref[...])
            l_ref[...] = jnp.where(lane == h, totals[i], l_ref[...])
            acc_ref[:, at] = jnp.where(own, mixes[i], acc_ref[:, at])

    head_groups(body)


def widen(factor, feature):
    head_size = feature // HEADS
    lane = lax.broadcasted_iota(jnp.int32, (1, LANES), 1)
    factor = jnp.where(lane < HEADS, factor, 0.0)
    high = factor.astype(jnp.bfloat16)
    low = (factor - high.astype(jnp.float32)).astype(jnp.bfloat16)
    head = lax.broadcasted_iota(jnp.int32, (2 * LANES, feature), 0) & (LANES - 1)
    column = lax.broadcasted_iota(jnp.int32, (2 * LANES, feature), 1)
    low_column = head * head_size
    owner = (column >= low_column) & (column < low_column + head_size)
    return jnp.dot(
        jnp.concatenate([high, low], axis=1),
        jnp.where(owner, 1.0, 0.0).astype(jnp.bfloat16),
        preferred_element_type=jnp.float32,
    )


def merge(m_ref, l_ref, acc_ref, m_new, l_new, acc_new):
    feature = acc_ref.shape[1]
    rate = (feature // HEADS) ** (-0.5) * LOG2E
    old, new = m_ref[...], m_new[...]
    top = jnp.maximum(old, new)
    fade_old = jnp.exp2((old - top) * rate)
    fade_new = jnp.exp2((new - top) * rate)
    m_ref[...] = top
    l_ref[...] = l_ref[...] * fade_old + l_new[...] * fade_new
    acc_ref[...] = acc_ref[...] * widen(fade_old, feature) + acc_new[...] * widen(
        fade_new, feature
    )


def compact_positions(keep):
    keys = keep.shape[1]
    row = lax.broadcasted_iota(jnp.int32, (keys, keys), 0)
    column = lax.broadcasted_iota(jnp.int32, (keys, keys), 1)
    upto = jnp.where(row <= column, 1.0, 0.0).astype(jnp.bfloat16)
    lines = jnp.broadcast_to(keep, (16, keys)).astype(jnp.bfloat16)
    return jnp.dot(lines, upto, preferred_element_type=jnp.float32)[:1]


def kept_keys(a_ref, b_ref):
    half = a_ref.shape[0] - STAMP
    flags = [ref[half:, :half].astype(jnp.float32)[:1] for ref in (a_ref, b_ref)]
    keep = jnp.concatenate([jnp.where(f == 0, 1.0, 0.0) for f in flags], axis=1)
    return keep, jnp.sum(keep).astype(jnp.int32)


def compact_block(b, keep, places, a_ref, b_ref, dst_ref):
    keys = keep.shape[1]
    half = keys // 2
    wanted = b * BLOCK + 1 + lax.broadcasted_iota(jnp.int32, (BLOCK, keys), 0)
    chosen = (places == wanted.astype(jnp.float32)) & (keep > 0)
    chosen = jnp.where(chosen, 1.0, 0.0).astype(jnp.bfloat16)
    dst_ref[...] = (
        jnp.dot(chosen[:, :half], a_ref[:half, :], preferred_element_type=jnp.float32)
        + jnp.dot(chosen[:, half:], b_ref[:half, :], preferred_element_type=jnp.float32)
    ).astype(jnp.bfloat16)


def tail_bias(b, count):
    slot = b * BLOCK + lax.broadcasted_iota(jnp.int32, (1, BLOCK), 1)
    return jnp.where(slot < count, 0.0, -jnp.inf)


def blocks_of(count):
    return (count + BLOCK - 1) // BLOCK


def stamp_kernel(x_ref, region_ref, ext_ref, first_ref):
    half, feature = x_ref.shape
    line = region_ref[...].astype(jnp.float32).astype(jnp.bfloat16)

    def fill(ref):
        ref[:half, :] = x_ref[...]
        ref[half:, :] = jnp.zeros((STAMP, feature), jnp.bfloat16)
        ref[half:, :half] = jnp.broadcast_to(line, (STAMP, half))

    fill(ext_ref)

    @pl.when(pl.program_id(0) == 0)
    def _():
        fill(first_ref)


def stamp(x, regions):
    frames, half, feature = x.shape
    return pl.pallas_call(
        stamp_kernel,
        name="stamp",
        grid=(frames,),
        in_specs=[
            pl.BlockSpec((None, half, feature), lambda f: (f, 0, 0)),
            pl.BlockSpec((None, 1, half), lambda f: (f, 0, 0)),
        ],
        out_specs=[
            pl.BlockSpec((None, half + STAMP, feature), lambda f: (f, 0, 0)),
            pl.BlockSpec((half + STAMP, feature), lambda f: (0, 0)),
        ],
        out_shape=[
            jax.ShapeDtypeStruct((frames, half + STAMP, feature), jnp.bfloat16),
            jax.ShapeDtypeStruct((half + STAMP, feature), jnp.bfloat16),
        ],
        compiler_params=params("arbitrary"),
    )(x, regions.reshape(frames, 1, half))


def own_project_kernel(xa_ref, xb_ref, gain_ref, w_ref, q_ref, kv_ref, normed, w_buf, sem):
    half, feature = xa_ref.shape
    copies = [
        pltpu.make_async_copy(
            w_ref.at[:, s * feature : (s + 1) * feature], w_buf.at[s], sem.at[s]
        )
        for s in range(3)
    ]
    first = pl.program_id(0) == 0

    @pl.when(first)
    def _():
        for copy in copies:
            copy.start()

    norm_rows(xa_ref, gain_ref, normed.at[:half])
    norm_rows(xb_ref.at[:half], gain_ref, normed.at[half:])
    for s in range(3):

        @pl.when(first)
        def _():
            copies[s].wait()

        if s == 0:
            project(normed.at[:half], w_buf.at[0], q_ref)
        else:
            project(normed, w_buf.at[s], kv_ref.at[s - 1])


def own_project(x_own, x_par, gain, weight):
    frames, half, feature = x_own.shape
    keys = 2 * half
    per_frame = pl.BlockSpec((None, half, feature), lambda f: (f, 0, 0))
    return pl.pallas_call(
        own_project_kernel,
        name="own_project",
        grid=(frames,),
        in_specs=[
            per_frame,
            pl.BlockSpec((None, half + STAMP, feature), lambda f: (f, 0, 0)),
            vmem(),
            whole(),
        ],
        out_specs=[per_frame, pl.BlockSpec((None, 2, keys, feature), lambda f: (f, 0, 0, 0))],
        out_shape=[
            jax.ShapeDtypeStruct((frames, half, feature), jnp.bfloat16),
            jax.ShapeDtypeStruct((frames, 2, keys, feature), jnp.bfloat16),
        ],
        scratch_shapes=[
            pltpu.VMEM((keys, feature), jnp.bfloat16),
            pltpu.VMEM((3, feature, feature), jnp.bfloat16),
            pltpu.SemaphoreType.DMA((3,)),
        ],
        cost_estimate=cost(8 * 10**9, 20 << 20),
        compiler_params=params("arbitrary"),
    )(x_own, x_par, gain, weight)


def own_kernel(q_ref, kv_ref, m_ref, l_ref, acc_ref):
    attend(q_ref, kv_ref.at[0], kv_ref.at[1], None, m_ref, l_ref, acc_ref)


def own_segment(q, kv):
    frames, half, feature = q.shape
    keys = kv.shape[2]
    per_frame = pl.BlockSpec((None, half, feature), lambda f: (f, 0, 0))
    column = pl.BlockSpec((None, half, LANES), lambda f: (f, 0, 0))
    return pl.pallas_call(
        own_kernel,
        name="own_segment",
        grid=(frames,),
        in_specs=[per_frame, pl.BlockSpec((None, 2, keys, feature), lambda f: (f, 0, 0, 0))],
        out_specs=[column, column, per_frame],
        out_shape=[
            jax.ShapeDtypeStruct((frames, half, LANES), jnp.float32),
            jax.ShapeDtypeStruct((frames, half, LANES), jnp.float32),
            jax.ShapeDtypeStruct((frames, half, feature), jnp.float32),
        ],
        cost_estimate=cost(5 * 10**9, 9 << 20),
        compiler_params=params("arbitrary"),
    )(q, kv)


def prev_kernel(
    prev_ref, tail_ref, tail_par_ref, own_ref, own_par_ref, gain_ref, w_ref,
    q_ref, m_in, l_in, acc_in, m_ref, l_ref, acc_ref,
    rows, packed, normed, kv, m_new, l_new, acc_new, w_buf, sem,
):
    feature = q_ref.shape[1]
    frames = own_ref.shape[0]
    base = lax.axis_index("frame") * frames
    f = pl.program_id(0)
    first = f == 0
    loads = [
        pltpu.make_async_copy(
            w_ref.at[:, (s + 1) * feature : (s + 2) * feature], w_buf.at[s], sem.at[s]
        )
        for s in range(2)
    ]

    @pl.when(first)
    def _():
        for copy in loads:
            copy.start()

    slot = prev_ref[base + f] - base + frames
    for pair, lowest in (((tail_ref, tail_par_ref), 0), ((own_ref, own_par_ref), frames)):
        here = (slot < frames) if lowest == 0 else (slot >= frames)

        @pl.when(here)
        def _(pair=pair, lowest=lowest):
            copies = [
                pltpu.make_async_copy(ref.at[slot - lowest], rows.at[t], sem.at[2 + t])
                for t, ref in enumerate(pair)
            ]
            for copy in copies:
                copy.start()
            for copy in copies:
                copy.wait()

    keep, count = kept_keys(rows.at[0], rows.at[1])
    places = compact_positions(keep)
    m_ref[...] = m_in[...]
    l_ref[...] = l_in[...]
    acc_ref[...] = acc_in[...]

    @pl.when(first)
    def _():
        for copy in loads:
            copy.wait()

    def block(b, carry):
        compact_block(b, keep, places, rows.at[0], rows.at[1], packed)
        norm_rows(packed, gain_ref, normed)
        for s in range(2):
            project(normed, w_buf.at[s], kv.at[s])
        attend(q_ref, kv.at[0], kv.at[1], tail_bias(b, count), m_new, l_new, acc_new)
        merge(m_ref, l_ref, acc_ref, m_new, l_new, acc_new)
        return carry

    lax.fori_loop(0, blocks_of(count), block, 0)


def prev_segment(prev, tail, tail_par, own, own_par, gain, weight, q, m, l, acc):
    frames, half, feature = q.shape
    per_frame = pl.BlockSpec((None, half, feature), lambda f: (f, 0, 0))
    column = pl.BlockSpec((None, half, LANES), lambda f: (f, 0, 0))
    return pl.pallas_call(
        prev_kernel,
        name="prev_segment",
        grid=(frames,),
        in_specs=[pl.BlockSpec(memory_space=pltpu.SMEM)]
        + [whole()] * 4
        + [vmem(), whole(), per_frame, column, column, per_frame],
        out_specs=[column, column, per_frame],
        out_shape=[
            jax.ShapeDtypeStruct(m.shape, jnp.float32),
            jax.ShapeDtypeStruct(l.shape, jnp.float32),
            jax.ShapeDtypeStruct(acc.shape, jnp.float32),
        ],
        scratch_shapes=[
            pltpu.VMEM((2, half + STAMP, feature), jnp.bfloat16),
            pltpu.VMEM((BLOCK, feature), jnp.bfloat16),
            pltpu.VMEM((BLOCK, feature), jnp.bfloat16),
            pltpu.VMEM((2, BLOCK, feature), jnp.bfloat16),
            pltpu.VMEM((half, LANES), jnp.float32),
            pltpu.VMEM((half, LANES), jnp.float32),
            pltpu.VMEM((half, feature), jnp.float32),
            pltpu.VMEM((2, feature, feature), jnp.bfloat16),
            pltpu.SemaphoreType.DMA((4,)),
        ],
        cost_estimate=cost(14 * 10**9, 16 << 20),
        compiler_params=params("arbitrary"),
    )(prev, tail, tail_par, own, own_par, gain, weight, q, m, l, acc)


def first_kv_kernel(xa_ref, xb_ref, gain_ref, w_ref, kv_ref, packed, normed, w_buf, sem):
    feature = xa_ref.shape[1]
    loads = [
        pltpu.make_async_copy(
            w_ref.at[:, (s + 1) * feature : (s + 2) * feature], w_buf.at[s], sem.at[s]
        )
        for s in range(2)
    ]
    for copy in loads:
        copy.start()
    keep, count = kept_keys(xa_ref, xb_ref)
    places = compact_positions(keep)

    def block(b, carry):
        compact_block(b, keep, places, xa_ref, xb_ref, packed)
        norm_rows(packed, gain_ref, normed)
        for s in range(2):

            @pl.when(b == 0)
            def _():
                loads[s].wait()

            project(normed, w_buf.at[s], kv_ref.at[s, b])
        return carry

    lax.fori_loop(0, blocks_of(count), block, 0)

    @pl.when(count == 0)
    def _():
        for copy in loads:
            copy.wait()


def first_kv(xa, xb, gain, weight):
    half, feature = xa.shape[0] - STAMP, xa.shape[1]
    return pl.pallas_call(
        first_kv_kernel,
        name="first_kv",
        in_specs=[vmem(), vmem(), vmem(), whole()],
        out_specs=vmem(),
        out_shape=jax.ShapeDtypeStruct((2, 2 * half // BLOCK, BLOCK, feature), jnp.bfloat16),
        scratch_shapes=[
            pltpu.VMEM((BLOCK, feature), jnp.bfloat16),
            pltpu.VMEM((BLOCK, feature), jnp.bfloat16),
            pltpu.VMEM((2, feature, feature), jnp.bfloat16),
            pltpu.SemaphoreType.DMA((2,)),
        ],
        cost_estimate=cost(3 * 10**9, 8 << 20),
        compiler_params=params(),
    )(xa, xb, gain, weight)


def last_kernel(
    xa_ref, xb_ref, kv_ref, q_ref, m_in, l_in, acc_in, x_ref, open_ref, w_ref, *refs
):
    frames, parties, piece, feature = x_ref.shape
    outs = refs[:parties]
    q_rows, m_rows, l_rows, acc_rows, m_new, l_new, acc_new, mixed, w_buf, sem = refs[parties:]
    rows = frames * parties * piece
    load = pltpu.make_async_copy(w_ref, w_buf, sem.at[0])
    load.start()
    q_rows[...] = q_ref[...].reshape(rows, feature)
    m_rows[...] = m_in[...].reshape(rows, LANES)
    l_rows[...] = l_in[...].reshape(rows, LANES)
    acc_rows[...] = acc_in[...].reshape(rows, feature)
    _, count = kept_keys(xa_ref, xb_ref)

    def block(b, carry):
        attend(
            q_rows, kv_ref.at[0, b], kv_ref.at[1, b], tail_bias(b, count), m_new, l_new, acc_new
        )
        merge(m_rows, l_rows, acc_rows, m_new, l_new, acc_new)
        return carry

    lax.fori_loop(0, blocks_of(count), block, 0)
    lane = lax.broadcasted_iota(jnp.int32, (1, LANES), 1)
    inverse = 1.0 / jnp.where(lane < HEADS, l_rows[...], 1.0)
    attended = (acc_rows[...] * widen(inverse, feature)).astype(jnp.bfloat16)
    load.wait()
    total = x_ref[...].reshape(rows, feature).astype(jnp.float32) + jnp.dot(
        attended, w_buf[...], preferred_element_type=jnp.float32
    )
    mixed[...] = total.astype(jnp.bfloat16).reshape(frames, parties, piece, feature)
    me = lax.axis_index("frame")
    for k in range(parties):
        outs[k][:, :, :feature] = mixed[:, lax.rem(me + k, parties)]
        outs[k][:, :, feature:] = open_ref[:, lax.rem(me + k, parties)]


def last_segment(xa, xb, kv, q, m, l, acc, x, opened, weight, parties, piece, chunk):
    frames, half, feature = q.shape
    chunks = half // (parties * piece)
    rows = frames * parties * piece

    def split(array):
        return array.reshape(frames, parties, chunks, piece, array.shape[-1])

    def spec(width):
        return pl.BlockSpec(
            (frames, parties, None, piece, width), lambda g: (0, 0, chunk, 0, 0)
        )

    return pl.pallas_call(
        last_kernel,
        name="last_segment",
        grid=(1,),
        in_specs=[vmem()] * 3
        + [spec(feature), spec(LANES), spec(LANES), spec(feature)]
        + [spec(feature), spec(LANES), whole()],
        out_specs=[vmem()] * parties,
        out_shape=[jax.ShapeDtypeStruct((frames, piece, feature + LANES), jnp.bfloat16)] * parties,
        scratch_shapes=[
            pltpu.VMEM((rows, feature), jnp.bfloat16),
            pltpu.VMEM((rows, LANES), jnp.float32),
            pltpu.VMEM((rows, LANES), jnp.float32),
            pltpu.VMEM((rows, feature), jnp.float32),
            pltpu.VMEM((rows, LANES), jnp.float32),
            pltpu.VMEM((rows, LANES), jnp.float32),
            pltpu.VMEM((rows, feature), jnp.float32),
            pltpu.VMEM((frames, parties, piece, feature), jnp.bfloat16),
            pltpu.VMEM((feature, feature), jnp.bfloat16),
            pltpu.SemaphoreType.DMA((1,)),
        ],
        cost_estimate=cost(4 * 10**9, 8 << 20),
        compiler_params=params("arbitrary"),
    )(
        xa, xb, kv, split(q), split(m), split(l), split(acc), split(x), split(opened), weight
    )


def temporal_kernel(parties, gain_ref, w_ref, out_w_ref, *refs):
    pieces = refs[:parties]
    outs = refs[parties : 2 * parties]
    rows_ref, normed, packed, bias, mix, w_buf, o_buf, sem = refs[2 * parties :]
    frames, piece, feature = outs[0].shape
    head_size = feature // HEADS
    rate = head_size ** (-0.5) * LOG2E
    step = frames * piece
    rows = parties * step
    copies = [
        pltpu.make_async_copy(
            w_ref.at[:, s * feature : (s + 1) * feature], w_buf.at[s], sem.at[s]
        )
        for s in range(3)
    ] + [pltpu.make_async_copy(out_w_ref, o_buf, sem.at[3])]
    for copy in copies:
        copy.start()
    for k in range(parties):
        rows_ref[k * step : (k + 1) * step, :] = pieces[k][...].reshape(step, feature + LANES)
    norm_rows(rows_ref.at[:, :feature], gain_ref, normed)
    lane = lax.broadcasted_iota(jnp.int32, (STAMP, LANES), 1)
    open_row = scores_of(
        jnp.where(lane == 0, 1.0, 0.0).astype(jnp.bfloat16), rows_ref[:, feature:]
    )[:1]
    row = lax.broadcasted_iota(jnp.int32, (rows, rows), 0)
    column = lax.broadcasted_iota(jnp.int32, (rows, rows), 1)
    same_place = (row & (piece - 1)) == (column & (piece - 1))
    seen = same_place & ((row == column) | (open_row > 0.5))
    bias[...] = jnp.where(seen, 0.0, -jnp.inf)
    for s in range(3):
        copies[s].wait()
        project(normed, w_buf.at[s], packed.at[s])

    def body(heads):
        views = [window(h, head_size) for h in heads]
        scores = [
            scores_of(jnp.where(own, packed[0, :, at], 0).astype(jnp.bfloat16), packed[1, :, at])
            + bias[...]
            for at, own in views
        ]
        tops = [jnp.max(s, axis=-1, keepdims=True) for s in scores]
        weights = [jnp.exp2((s - t) * rate) for s, t in zip(scores, tops)]
        totals = [jnp.sum(w, axis=-1, keepdims=True) for w in weights]
        gots = [
            jnp.dot(w.astype(jnp.bfloat16), packed[2, :, at], preferred_element_type=jnp.float32)
            for w, (at, _) in zip(weights, views)
        ]
        for (at, own), got, total in zip(views, gots, totals):
            done = (got * (1.0 / total)).astype(jnp.bfloat16)
            mix[:, at] = jnp.where(own, done, mix[:, at])

    head_groups(body)
    copies[3].wait()
    result = rows_ref[:, :feature].astype(jnp.float32) + jnp.dot(
        mix[...], o_buf[...], preferred_element_type=jnp.float32
    )
    result = result.astype(jnp.bfloat16)
    for k in range(parties):
        outs[k][...] = result[k * step : (k + 1) * step, :].reshape(frames, piece, feature)


def temporal_block(pieces, gain, weight, out_weight):
    parties = len(pieces)
    frames, piece, wide = pieces[0].shape
    feature = weight.shape[0]
    rows = parties * frames * piece
    return pl.pallas_call(
        functools.partial(temporal_kernel, parties),
        name="temporal_block",
        in_specs=[vmem(), whole(), whole()] + [vmem()] * parties,
        out_specs=[vmem()] * parties,
        out_shape=[jax.ShapeDtypeStruct((frames, piece, feature), jnp.bfloat16)] * parties,
        scratch_shapes=[
            pltpu.VMEM((rows, wide), jnp.bfloat16),
            pltpu.VMEM((rows, feature), jnp.bfloat16),
            pltpu.VMEM((3, rows, feature), jnp.bfloat16),
            pltpu.VMEM((rows, rows), jnp.float32),
            pltpu.VMEM((rows, feature), jnp.bfloat16),
            pltpu.VMEM((3, feature, feature), jnp.bfloat16),
            pltpu.VMEM((feature, feature), jnp.bfloat16),
            pltpu.SemaphoreType.DMA((4,)),
        ],
        cost_estimate=cost(6 * 10**9, 12 << 20),
        compiler_params=params(),
    )(gain, weight, out_weight, *pieces)


def gather_kernel(chunks, parties, *refs):
    out_ref = refs[-1]
    me = lax.axis_index("frame")
    for c in range(chunks):
        for k in range(parties):
            out_ref[:, lax.rem(me + k, parties), c] = refs[c * parties + k][...]


def gather_pieces(pieces, chunks, parties):
    frames, piece, feature = pieces[0].shape
    shape = (frames, parties, chunks, piece, feature)
    out = pl.pallas_call(
        functools.partial(gather_kernel, chunks, parties),
        name="gather_pieces",
        in_specs=[vmem()] * len(pieces),
        out_specs=vmem(),
        out_shape=jax.ShapeDtypeStruct(shape, jnp.bfloat16),
        compiler_params=params(),
    )(*pieces)
    return out.reshape(frames, parties * chunks * piece, feature)


def swap(array, axis):
    count = lax.axis_size(axis)
    return lax.ppermute(array, axis, [(i, count - 1 - i) for i in range(count)])


def shards(
    video,
    regions,
    prev_frame,
    gain_spatial,
    qkv_spatial,
    out_spatial,
    gain_temporal,
    qkv_temporal,
    out_temporal,
):
    frames, half, feature = video.shape
    parties = lax.axis_size("frame")
    me = lax.axis_index("frame")
    gain_s = gain_spatial.reshape(1, feature)
    gain_t = gain_temporal.reshape(1, feature)

    ext, x_first = stamp(video, regions)

    x_par = swap(ext, "tok")
    forward = [(i, i + 1) for i in range(parties - 1)]
    tail = lax.ppermute(ext, "frame", forward)
    tail_par = swap(tail, "tok")
    for stride in strides_of(parties):
        pairs = [(j, j + stride) for j in range(0, parties, 2 * stride)]
        got = lax.ppermute(x_first, "frame", pairs)
        x_first = jnp.where(me % (2 * stride) == stride, got, x_first)
    first_par = swap(x_first, "tok")

    q, kv_own = own_project(video, x_par, gain_s, qkv_spatial)
    m, l, acc = own_segment(q, kv_own)
    m, l, acc = prev_segment(
        prev_frame, tail, tail_par, ext, x_par, gain_s, qkv_spatial, q, m, l, acc
    )
    kv = first_kv(x_first, first_par, gain_s, qkv_spatial)
    opened = jnp.broadcast_to((regions != 2)[..., None], (frames, half, LANES))
    opened = opened.astype(jnp.bfloat16)

    chunks = half // (parties * PIECE_ROWS)

    def shift(array, k):
        return lax.ppermute(
            array, "frame", [(j, (j + k) % parties) for j in range(parties)]
        )

    returned = []
    for c in range(chunks):
        sent = last_segment(
            x_first, first_par, kv, q, m, l, acc, video, opened, out_spatial,
            parties, PIECE_ROWS, c,
        )
        got = [sent[0]] + [shift(sent[k], k) for k in range(1, parties)]
        back = temporal_block(got, gain_t, qkv_temporal, out_temporal)
        returned += [back[0]] + [shift(back[k], -k) for k in range(1, parties)]
    return gather_pieces(returned, chunks, parties)


def strides_of(parties):
    strides = []
    while parties > 1:
        parties //= 2
        strides.append(parties)
    return strides


def solution(mesh):
    placed = (
        P(("groups", "frame"), "tok", None),
        P(("groups", "frame"), "tok"),
        P("groups"),
        P(),
        P(),
        P(),
        P(),
        P(),
        P(),
    )
    return jax.shard_map(
        shards,
        mesh=mesh,
        in_specs=placed,
        out_specs=P(("groups", "frame"), "tok", None),
        check_vma=False,
    )
```

```python
import functools

import jax
import jax.numpy as jnp
from jax import lax
from jax.experimental import pallas as pl
from jax.experimental.pallas import tpu as pltpu
from jax.sharding import PartitionSpec as P


HEADS = 16
BLOCK = 256
GROUP = 4
LANES = 128
PIECE_ROWS = 16
STAMP = 16
GRANT = 24 << 20
LOG2E = 1.4426950408889634


def vmem():
    return pl.BlockSpec(memory_space=pltpu.VMEM)


def whole():
    return pl.BlockSpec(memory_space=pl.ANY)


def in_hbm():
    return pl.BlockSpec(memory_space=pltpu.HBM)


def params(*semantics):
    return pltpu.CompilerParams(
        dimension_semantics=semantics or None, vmem_limit_bytes=GRANT
    )


def cost(flops, moved):
    return pl.CostEstimate(flops=flops, transcendentals=0, bytes_accessed=moved)


def norm_rows(src_ref, gain_ref, dst_ref, block=32):
    rows, feature = src_ref.shape
    gain = gain_ref[...].reshape(1, feature)

    def step(r, carry):
        at = pl.ds(pl.multiple_of(r * block, block), block)
        values = src_ref[at, :].astype(jnp.float32)
        center = values - jnp.mean(values, axis=-1, keepdims=True)
        spread = jnp.mean(center * center, axis=-1, keepdims=True)
        dst_ref[at, :] = (center * lax.rsqrt(spread + 1e-06) * gain).astype(jnp.bfloat16)
        return carry

    lax.fori_loop(0, rows // block, step, 0, unroll=4)


def project(src, count, source, target, ready=None):
    def part(s, carry):
        if ready is not None:
            ready(s)
        target(s)[...] = jnp.dot(
            src[...], source(s)[...], preferred_element_type=jnp.float32
        ).astype(jnp.bfloat16)
        return carry

    lax.fori_loop(0, count, part, 0)


def part_loads(w_ref, w_buf, sem, lead):
    parts, feature = w_buf.shape[0], w_buf.shape[1]

    def load(s):
        at = pl.multiple_of((s + lead) * feature, LANES)
        return pltpu.make_async_copy(
            w_ref.at[:, pl.ds(at, feature)], w_buf.at[s], sem.at[s]
        )

    def start():
        for s in range(parts):
            load(s).start()

    return start, lambda s: load(s).wait()


def window(h, head_size):
    low, high = h * head_size, (h + 1) * head_size
    start = low // LANES * LANES
    stop = pl.cdiv(high, LANES) * LANES
    lane = start + lax.broadcasted_iota(jnp.int32, (1, stop - start), 1)
    return slice(start, stop), (lane >= low) & (lane < high)


def scores_of(query, key):
    return lax.dot_general(
        query, key, (((1,), (1,)), ((), ())), preferred_element_type=jnp.float32
    )


def head_groups(body):
    for first in range(0, HEADS, GROUP):
        body(range(first, first + GROUP))


def attend(q_ref, k_ref, v_ref, bias, m_ref, l_ref, acc_ref):
    head_size = q_ref.shape[1] // HEADS
    rate = head_size ** (-0.5) * LOG2E
    lane = lax.broadcasted_iota(jnp.int32, (1, LANES), 1)

    def body(heads):
        views = [window(h, head_size) for h in heads]
        scores = [
            scores_of(jnp.where(own, q_ref[:, at], 0).astype(jnp.bfloat16), k_ref[:, at])
            for at, own in views
        ]
        if bias is not None:
            scores = [s + bias for s in scores]
        tops = [jnp.max(s, axis=-1, keepdims=True) for s in scores]
        weights = [jnp.exp2((s - t) * rate) for s, t in zip(scores, tops)]
        totals = [jnp.sum(w, axis=-1, keepdims=True) for w in weights]
        mixes = [
            jnp.dot(w.astype(jnp.bfloat16), v_ref[:, at], preferred_element_type=jnp.float32)
            for w, (at, _) in zip(weights, views)
        ]
        for i, h in enumerate(heads):
            at, own = views[i]
            m_ref[...] = jnp.where(lane == h, tops[i], m_ref[...])
            l_ref[...] = jnp.where(lane == h, totals[i], l_ref[...])
            acc_ref[:, at] = jnp.where(own, mixes[i], acc_ref[:, at])

    head_groups(body)


def widen(factor, feature):
    head_size = feature // HEADS
    lane = lax.broadcasted_iota(jnp.int32, (1, LANES), 1)
    factor = jnp.where(lane < HEADS, factor, 0.0)
    high = factor.astype(jnp.bfloat16)
    low = (factor - high.astype(jnp.float32)).astype(jnp.bfloat16)
    head = lax.broadcasted_iota(jnp.int32, (2 * LANES, feature), 0) & (LANES - 1)
    column = lax.broadcasted_iota(jnp.int32, (2 * LANES, feature), 1)
    low_column = head * head_size
    owner = (column >= low_column) & (column < low_column + head_size)
    return jnp.dot(
        jnp.concatenate([high, low], axis=1),
        jnp.where(owner, 1.0, 0.0).astype(jnp.bfloat16),
        preferred_element_type=jnp.float32,
    )


def merge(m_ref, l_ref, acc_ref, m_new, l_new, acc_new):
    feature = acc_ref.shape[1]
    rate = (feature // HEADS) ** (-0.5) * LOG2E
    old, new = m_ref[...], m_new[...]
    top = jnp.maximum(old, new)
    fade_old = jnp.exp2((old - top) * rate)
    fade_new = jnp.exp2((new - top) * rate)
    m_ref[...] = top
    l_ref[...] = l_ref[...] * fade_old + l_new[...] * fade_new
    acc_ref[...] = acc_ref[...] * widen(fade_old, feature) + acc_new[...] * widen(
        fade_new, feature
    )


def compact_positions(keep):
    keys = keep.shape[1]
    row = lax.broadcasted_iota(jnp.int32, (keys, keys), 0)
    column = lax.broadcasted_iota(jnp.int32, (keys, keys), 1)
    upto = jnp.where(row <= column, 1.0, 0.0).astype(jnp.bfloat16)
    lines = jnp.broadcast_to(keep, (16, keys)).astype(jnp.bfloat16)
    return jnp.dot(lines, upto, preferred_element_type=jnp.float32)[:1]


def kept_keys(a_ref, b_ref):
    half = a_ref.shape[0] - STAMP
    flags = [ref[half:, :half].astype(jnp.float32)[:1] for ref in (a_ref, b_ref)]
    keep = jnp.concatenate([jnp.where(f == 0, 1.0, 0.0) for f in flags], axis=1)
    return keep, jnp.sum(keep).astype(jnp.int32)


def compact_block(b, keep, places, a_ref, b_ref, dst_ref):
    keys = keep.shape[1]
    half = keys // 2
    wanted = b * BLOCK + 1 + lax.broadcasted_iota(jnp.int32, (BLOCK, keys), 0)
    chosen = (places == wanted.astype(jnp.float32)) & (keep > 0)
    chosen = jnp.where(chosen, 1.0, 0.0).astype(jnp.bfloat16)
    dst_ref[...] = (
        jnp.dot(chosen[:, :half], a_ref[:half, :], preferred_element_type=jnp.float32)
        + jnp.dot(chosen[:, half:], b_ref[:half, :], preferred_element_type=jnp.float32)
    ).astype(jnp.bfloat16)


def tail_bias(b, count):
    slot = b * BLOCK + lax.broadcasted_iota(jnp.int32, (1, BLOCK), 1)
    return jnp.where(slot < count, 0.0, -jnp.inf)


def blocks_of(count):
    return (count + BLOCK - 1) // BLOCK


def stamp_kernel(x_ref, region_ref, ext_ref, first_ref):
    half, feature = x_ref.shape
    line = region_ref[pl.ds(pl.program_id(0), 1), :].astype(jnp.float32).astype(jnp.bfloat16)

    def fill(ref):
        ref[:half, :] = x_ref[...]
        ref[half:, :] = jnp.zeros((STAMP, feature), jnp.bfloat16)
        ref[half:, :half] = jnp.broadcast_to(line, (STAMP, half))

    fill(ext_ref)

    @pl.when(pl.program_id(0) == 0)
    def _():
        fill(first_ref)


def stamp(x, regions):
    frames, half, feature = x.shape
    return pl.pallas_call(
        stamp_kernel,
        name="stamp",
        grid=(frames,),
        in_specs=[
            pl.BlockSpec((None, half, feature), lambda f: (f, 0, 0)),
            vmem(),
        ],
        out_specs=[
            pl.BlockSpec((None, half + STAMP, feature), lambda f: (f, 0, 0)),
            pl.BlockSpec((half + STAMP, feature), lambda f: (0, 0)),
        ],
        out_shape=[
            jax.ShapeDtypeStruct((frames, half + STAMP, feature), jnp.bfloat16),
            jax.ShapeDtypeStruct((half + STAMP, feature), jnp.bfloat16),
        ],
        compiler_params=params("arbitrary"),
    )(x, regions)


def own_project_kernel(xa_ref, xb_ref, gain_ref, w_ref, q_ref, kv_ref, normed, w_buf, sem):
    half, _ = xa_ref.shape
    start, wait = part_loads(w_ref, w_buf, sem, 0)
    first = pl.program_id(0) == 0

    @pl.when(first)
    def _():
        start()

    def ready(s):
        @pl.when(first)
        def _():
            wait(s)

    norm_rows(xa_ref, gain_ref, normed.at[:half])
    norm_rows(xb_ref.at[:half], gain_ref, normed.at[half:])
    ready(0)
    q_ref[...] = jnp.dot(
        normed[:half, :], w_buf[0], preferred_element_type=jnp.float32
    ).astype(jnp.bfloat16)
    project(
        normed, 2, lambda s: w_buf.at[s + 1], lambda s: kv_ref.at[s], lambda s: ready(s + 1)
    )


def own_project(x_own, x_par, gain, weight):
    frames, half, feature = x_own.shape
    keys = 2 * half
    per_frame = pl.BlockSpec((None, half, feature), lambda f: (f, 0, 0))
    return pl.pallas_call(
        own_project_kernel,
        name="own_project",
        grid=(frames,),
        in_specs=[
            per_frame,
            pl.BlockSpec((None, half + STAMP, feature), lambda f: (f, 0, 0)),
            vmem(),
            in_hbm(),
        ],
        out_specs=[per_frame, pl.BlockSpec((None, 2, keys, feature), lambda f: (f, 0, 0, 0))],
        out_shape=[
            jax.ShapeDtypeStruct((frames, half, feature), jnp.bfloat16),
            jax.ShapeDtypeStruct((frames, 2, keys, feature), jnp.bfloat16),
        ],
        scratch_shapes=[
            pltpu.VMEM((keys, feature), jnp.bfloat16),
            pltpu.VMEM((3, feature, feature), jnp.bfloat16),
            pltpu.SemaphoreType.DMA((3,)),
        ],
        cost_estimate=cost(8 * 10**9, 20 << 20),
        compiler_params=params("arbitrary"),
    )(x_own, x_par, gain, weight)


def own_kernel(q_ref, kv_ref, region_ref, m_ref, l_ref, acc_ref, open_ref):
    half = q_ref.shape[0]
    line = region_ref[pl.ds(pl.program_id(0), 1), :]
    line = jnp.broadcast_to(jnp.where(line == 2, 0.0, 1.0), (LANES, half)).astype(jnp.bfloat16)
    row = lax.broadcasted_iota(jnp.int32, (half, half), 0)
    column = lax.broadcasted_iota(jnp.int32, (half, half), 1)
    same = jnp.where(row == column, 1.0, 0.0).astype(jnp.bfloat16)
    open_ref[...] = scores_of(same, line).astype(jnp.bfloat16)
    attend(q_ref, kv_ref.at[0], kv_ref.at[1], None, m_ref, l_ref, acc_ref)


def own_segment(q, kv, regions):
    frames, half, feature = q.shape
    keys = kv.shape[2]
    per_frame = pl.BlockSpec((None, half, feature), lambda f: (f, 0, 0))
    column = pl.BlockSpec((None, half, LANES), lambda f: (f, 0, 0))
    return pl.pallas_call(
        own_kernel,
        name="own_segment",
        grid=(frames,),
        in_specs=[
            per_frame,
            pl.BlockSpec((None, 2, keys, feature), lambda f: (f, 0, 0, 0)),
            vmem(),
        ],
        out_specs=[column, column, per_frame, column],
        out_shape=[
            jax.ShapeDtypeStruct((frames, half, LANES), jnp.float32),
            jax.ShapeDtypeStruct((frames, half, LANES), jnp.float32),
            jax.ShapeDtypeStruct((frames, half, feature), jnp.float32),
            jax.ShapeDtypeStruct((frames, half, LANES), jnp.bfloat16),
        ],
        cost_estimate=cost(5 * 10**9, 9 << 20),
        compiler_params=params("arbitrary"),
    )(q, kv, regions)


def prev_kernel(
    prev_ref, tail_ref, tail_par_ref, own_ref, own_par_ref, gain_ref, w_ref,
    q_ref, m_in, l_in, acc_in, m_ref, l_ref, acc_ref,
    rows, packed, normed, kv, m_new, l_new, acc_new, w_buf, w_sem, sem,
):
    frames = own_ref.shape[0]
    base = lax.axis_index("frame") * frames
    f = pl.program_id(0)
    start, wait = part_loads(w_ref, w_buf, w_sem, 1)

    @pl.when(f == 0)
    def _():
        start()

    slot = prev_ref[base + f] - base + frames
    for pair, lowest in (((tail_ref, tail_par_ref), 0), ((own_ref, own_par_ref), frames)):
        here = (slot < frames) if lowest == 0 else (slot >= frames)

        @pl.when(here)
        def _(pair=pair, lowest=lowest):
            copies = [
                pltpu.make_async_copy(ref.at[slot - lowest], rows.at[t], sem.at[t])
                for t, ref in enumerate(pair)
            ]
            for copy in copies:
                copy.start()
            for copy in copies:
                copy.wait()

    keep, count = kept_keys(rows.at[0], rows.at[1])
    places = compact_positions(keep)
    m_ref[...] = m_in[...]
    l_ref[...] = l_in[...]
    acc_ref[...] = acc_in[...]

    def block(b, carry):
        compact_block(b, keep, places, rows.at[0], rows.at[1], packed)
        norm_rows(packed, gain_ref, normed)

        def ready(s):
            @pl.when((f == 0) & (b == 0))
            def _():
                wait(s)

        project(normed, 2, lambda s: w_buf.at[s], lambda s: kv.at[s], ready)
        attend(q_ref, kv.at[0], kv.at[1], tail_bias(b, count), m_new, l_new, acc_new)
        merge(m_ref, l_ref, acc_ref, m_new, l_new, acc_new)
        return carry

    lax.fori_loop(0, blocks_of(count), block, 0)

    @pl.when((f == 0) & (count == 0))
    def _():
        for s in range(2):
            wait(s)


def prev_segment(prev, tail, tail_par, own, own_par, gain, weight, q, m, l, acc):
    frames, half, feature = q.shape
    per_frame = pl.BlockSpec((None, half, feature), lambda f: (f, 0, 0))
    column = pl.BlockSpec((None, half, LANES), lambda f: (f, 0, 0))
    return pl.pallas_call(
        prev_kernel,
        name="prev_segment",
        grid=(frames,),
        in_specs=[pl.BlockSpec(memory_space=pltpu.SMEM)]
        + [whole()] * 4
        + [vmem(), in_hbm(), per_frame, column, column, per_frame],
        out_specs=[column, column, per_frame],
        out_shape=[
            jax.ShapeDtypeStruct(m.shape, jnp.float32),
            jax.ShapeDtypeStruct(l.shape, jnp.float32),
            jax.ShapeDtypeStruct(acc.shape, jnp.float32),
        ],
        scratch_shapes=[
            pltpu.VMEM((2, half + STAMP, feature), jnp.bfloat16),
            pltpu.VMEM((BLOCK, feature), jnp.bfloat16),
            pltpu.VMEM((BLOCK, feature), jnp.bfloat16),
            pltpu.VMEM((2, BLOCK, feature), jnp.bfloat16),
            pltpu.VMEM((half, LANES), jnp.float32),
            pltpu.VMEM((half, LANES), jnp.float32),
            pltpu.VMEM((half, feature), jnp.float32),
            pltpu.VMEM((2, feature, feature), jnp.bfloat16),
            pltpu.SemaphoreType.DMA((2,)),
            pltpu.SemaphoreType.DMA((2,)),
        ],
        cost_estimate=cost(14 * 10**9, 16 << 20),
        compiler_params=params("arbitrary"),
    )(prev, tail, tail_par, own, own_par, gain, weight, q, m, l, acc)


def first_kv_kernel(xa_ref, xb_ref, gain_ref, w_ref, kv_ref, packed, normed, w_buf, sem):
    start, wait = part_loads(w_ref, w_buf, sem, 1)
    start()
    keep, count = kept_keys(xa_ref, xb_ref)
    places = compact_positions(keep)

    def block(b, carry):
        compact_block(b, keep, places, xa_ref, xb_ref, packed)
        norm_rows(packed, gain_ref, normed)

        def ready(s):
            @pl.when(b == 0)
            def _():
                wait(s)

        project(normed, 2, lambda s: w_buf.at[s], lambda s: kv_ref.at[s, b], ready)
        return carry

    lax.fori_loop(0, blocks_of(count), block, 0)

    @pl.when(count == 0)
    def _():
        for s in range(2):
            wait(s)


def first_kv(xa, xb, gain, weight):
    half, feature = xa.shape[0] - STAMP, xa.shape[1]
    return pl.pallas_call(
        first_kv_kernel,
        name="first_kv",
        in_specs=[vmem(), vmem(), vmem(), in_hbm()],
        out_specs=vmem(),
        out_shape=jax.ShapeDtypeStruct((2, 2 * half // BLOCK, BLOCK, feature), jnp.bfloat16),
        scratch_shapes=[
            pltpu.VMEM((BLOCK, feature), jnp.bfloat16),
            pltpu.VMEM((BLOCK, feature), jnp.bfloat16),
            pltpu.VMEM((2, feature, feature), jnp.bfloat16),
            pltpu.SemaphoreType.DMA((2,)),
        ],
        cost_estimate=cost(3 * 10**9, 8 << 20),
        compiler_params=params(),
    )(xa, xb, gain, weight)


def last_kernel(
    xa_ref, xb_ref, kv_ref, q_ref, m_in, l_in, acc_in, x_ref, open_ref, w_ref, *refs
):
    frames, parties, piece, feature = x_ref.shape
    outs = refs[:parties]
    q_rows, m_rows, l_rows, acc_rows, m_new, l_new, acc_new, mixed = refs[parties:]
    rows = frames * parties * piece
    q_rows[...] = q_ref[...].reshape(rows, feature)
    m_rows[...] = m_in[...].reshape(rows, LANES)
    l_rows[...] = l_in[...].reshape(rows, LANES)
    acc_rows[...] = acc_in[...].reshape(rows, feature)
    _, count = kept_keys(xa_ref, xb_ref)

    def block(b, carry):
        attend(
            q_rows, kv_ref.at[0, b], kv_ref.at[1, b], tail_bias(b, count), m_new, l_new, acc_new
        )
        merge(m_rows, l_rows, acc_rows, m_new, l_new, acc_new)
        return carry

    lax.fori_loop(0, blocks_of(count), block, 0)
    lane = lax.broadcasted_iota(jnp.int32, (1, LANES), 1)
    inverse = 1.0 / jnp.where(lane < HEADS, l_rows[...], 1.0)
    attended = (acc_rows[...] * widen(inverse, feature)).astype(jnp.bfloat16)
    total = x_ref[...].reshape(rows, feature).astype(jnp.float32) + jnp.dot(
        attended, w_ref[...], preferred_element_type=jnp.float32
    )
    mixed[...] = total.astype(jnp.bfloat16).reshape(frames, parties, piece, feature)
    me = lax.axis_index("frame")
    for k in range(parties):
        outs[k][:, :, :feature] = mixed[:, lax.rem(me + k, parties)]
        outs[k][:, :, feature:] = open_ref[:, lax.rem(me + k, parties)]


def last_segment(xa, xb, kv, q, m, l, acc, x, opened, weight, parties, piece, chunk):
    frames, half, feature = q.shape
    chunks = half // (parties * piece)
    rows = frames * parties * piece

    def split(array):
        return array.reshape(frames, parties, chunks, piece, array.shape[-1])

    def spec(width):
        return pl.BlockSpec(
            (frames, parties, None, piece, width), lambda g: (0, 0, chunk, 0, 0)
        )

    return pl.pallas_call(
        last_kernel,
        name="last_segment",
        grid=(1,),
        in_specs=[vmem()] * 3
        + [spec(feature), spec(LANES), spec(LANES), spec(feature)]
        + [spec(feature), spec(LANES), vmem()],
        out_specs=[vmem()] * parties,
        out_shape=[jax.ShapeDtypeStruct((frames, piece, feature + LANES), jnp.bfloat16)] * parties,
        scratch_shapes=[
            pltpu.VMEM((rows, feature), jnp.bfloat16),
            pltpu.VMEM((rows, LANES), jnp.float32),
            pltpu.VMEM((rows, LANES), jnp.float32),
            pltpu.VMEM((rows, feature), jnp.float32),
            pltpu.VMEM((rows, LANES), jnp.float32),
            pltpu.VMEM((rows, LANES), jnp.float32),
            pltpu.VMEM((rows, feature), jnp.float32),
            pltpu.VMEM((frames, parties, piece, feature), jnp.bfloat16),
        ],
        cost_estimate=cost(4 * 10**9, 8 << 20),
        compiler_params=params("arbitrary"),
    )(
        xa, xb, kv, split(q), split(m), split(l), split(acc), split(x), split(opened), weight
    )


def temporal_kernel(parties, gain_ref, w_ref, out_w_ref, *refs):
    pieces = refs[:parties]
    outs = refs[parties : 2 * parties]
    rows_ref, normed, packed, bias, mix = refs[2 * parties :]
    frames, piece, feature = outs[0].shape
    head_size = feature // HEADS
    rate = head_size ** (-0.5) * LOG2E
    step = frames * piece
    rows = parties * step
    for k in range(parties):
        rows_ref[k * step : (k + 1) * step, :] = pieces[k][...].reshape(step, feature + LANES)
    norm_rows(rows_ref.at[:, :feature], gain_ref, normed)
    lane = lax.broadcasted_iota(jnp.int32, (STAMP, LANES), 1)
    open_row = scores_of(
        jnp.where(lane == 0, 1.0, 0.0).astype(jnp.bfloat16), rows_ref[:, feature:]
    )[:1]
    row = lax.broadcasted_iota(jnp.int32, (rows, rows), 0)
    column = lax.broadcasted_iota(jnp.int32, (rows, rows), 1)
    same_place = (row & (piece - 1)) == (column & (piece - 1))
    seen = same_place & ((row == column) | (open_row > 0.5))
    bias[...] = jnp.where(seen, 0.0, -jnp.inf)
    project(
        normed,
        3,
        lambda s: w_ref.at[:, pl.ds(pl.multiple_of(s * feature, LANES), feature)],
        lambda s: packed.at[s],
    )

    def body(heads):
        views = [window(h, head_size) for h in heads]
        scores = [
            scores_of(jnp.where(own, packed[0, :, at], 0).astype(jnp.bfloat16), packed[1, :, at])
            + bias[...]
            for at, own in views
        ]
        tops = [jnp.max(s, axis=-1, keepdims=True) for s in scores]
        weights = [jnp.exp2((s - t) * rate) for s, t in zip(scores, tops)]
        totals = [jnp.sum(w, axis=-1, keepdims=True) for w in weights]
        gots = [
            jnp.dot(w.astype(jnp.bfloat16), packed[2, :, at], preferred_element_type=jnp.float32)
            for w, (at, _) in zip(weights, views)
        ]
        for (at, own), got, total in zip(views, gots, totals):
            done = (got * (1.0 / total)).astype(jnp.bfloat16)
            mix[:, at] = jnp.where(own, done, mix[:, at])

    head_groups(body)
    result = rows_ref[:, :feature].astype(jnp.float32) + jnp.dot(
        mix[...], out_w_ref[...], preferred_element_type=jnp.float32
    )
    result = result.astype(jnp.bfloat16)
    for k in range(parties):
        outs[k][...] = result[k * step : (k + 1) * step, :].reshape(frames, piece, feature)


def temporal_block(pieces, gain, weight, out_weight):
    parties = len(pieces)
    frames, piece, wide = pieces[0].shape
    feature = weight.shape[0]
    rows = parties * frames * piece
    return pl.pallas_call(
        functools.partial(temporal_kernel, parties),
        name="temporal_block",
        in_specs=[vmem()] * (parties + 3),
        out_specs=[vmem()] * parties,
        out_shape=[jax.ShapeDtypeStruct((frames, piece, feature), jnp.bfloat16)] * parties,
        scratch_shapes=[
            pltpu.VMEM((rows, wide), jnp.bfloat16),
            pltpu.VMEM((rows, feature), jnp.bfloat16),
            pltpu.VMEM((3, rows, feature), jnp.bfloat16),
            pltpu.VMEM((rows, rows), jnp.float32),
            pltpu.VMEM((rows, feature), jnp.bfloat16),
        ],
        cost_estimate=cost(6 * 10**9, 12 << 20),
        compiler_params=params(),
    )(gain, weight, out_weight, *pieces)


def gather_kernel(chunks, parties, *refs):
    out_ref = refs[-1]
    me = lax.axis_index("frame")
    for c in range(chunks):
        for k in range(parties):
            out_ref[:, lax.rem(me + k, parties), c] = refs[c * parties + k][...]


def gather_pieces(pieces, chunks, parties):
    frames, piece, feature = pieces[0].shape
    shape = (frames, parties, chunks, piece, feature)
    out = pl.pallas_call(
        functools.partial(gather_kernel, chunks, parties),
        name="gather_pieces",
        in_specs=[vmem()] * len(pieces),
        out_specs=vmem(),
        out_shape=jax.ShapeDtypeStruct(shape, jnp.bfloat16),
        compiler_params=params(),
    )(*pieces)
    return out.reshape(frames, parties * chunks * piece, feature)


def swap(array, axis):
    count = lax.axis_size(axis)
    return lax.ppermute(array, axis, [(i, count - 1 - i) for i in range(count)])


def shards(
    video,
    regions,
    prev_frame,
    gain_spatial,
    qkv_spatial,
    out_spatial,
    gain_temporal,
    qkv_temporal,
    out_temporal,
):
    _, half, _ = video.shape
    parties = lax.axis_size("frame")
    me = lax.axis_index("frame")
    gain_s, gain_t = gain_spatial, gain_temporal
    qkv_spatial = pltpu.with_memory_space_constraint(qkv_spatial, pltpu.HBM)

    ext, x_first = stamp(video, regions)

    x_par = swap(ext, "tok")
    forward = [(i, i + 1) for i in range(parties - 1)]
    tail = lax.ppermute(ext, "frame", forward)
    tail_par = swap(tail, "tok")
    for stride in strides_of(parties):
        pairs = [(j, j + stride) for j in range(0, parties, 2 * stride)]
        got = lax.ppermute(x_first, "frame", pairs)
        x_first = jnp.where(me % (2 * stride) == stride, got, x_first)
    first_par = swap(x_first, "tok")

    q, kv_own = own_project(video, x_par, gain_s, qkv_spatial)
    m, l, acc, opened = own_segment(q, kv_own, regions)
    m, l, acc = prev_segment(
        prev_frame, tail, tail_par, ext, x_par, gain_s, qkv_spatial, q, m, l, acc
    )
    kv = first_kv(x_first, first_par, gain_s, qkv_spatial)

    chunks = half // (parties * PIECE_ROWS)

    def shift(array, k):
        return lax.ppermute(
            array, "frame", [(j, (j + k) % parties) for j in range(parties)]
        )

    returned = []
    for c in range(chunks):
        sent = last_segment(
            x_first, first_par, kv, q, m, l, acc, video, opened, out_spatial,
            parties, PIECE_ROWS, c,
        )
        got = [sent[0]] + [shift(sent[k], k) for k in range(1, parties)]
        back = temporal_block(got, gain_t, qkv_temporal, out_temporal)
        returned += [back[0]] + [shift(back[k], -k) for k in range(1, parties)]
    return gather_pieces(returned, chunks, parties)


def strides_of(parties):
    strides = []
    while parties > 1:
        parties //= 2
        strides.append(parties)
    return strides


def solution(mesh):
    placed = (
        P(("groups", "frame"), "tok", None),
        P(("groups", "frame"), "tok"),
        P("groups"),
        P(),
        P(),
        P(),
        P(),
        P(),
        P(),
    )
    return jax.shard_map(
        shards,
        mesh=mesh,
        in_specs=placed,
        out_specs=P(("groups", "frame"), "tok", None),
        check_vma=False,
    )
```
